32 devices in a mesh: seq: 8 (over z, y), head: 4 (over x, core).
Axes of the slice: x: 2, y: 2, z: 4, core: 2. Of those that a mesh axis runs over, the one named last changes fastest.
Arguments:
- tokens: bfloat16 [8192, 2048], P('seq'), may hold values from -6 to 6
- w_query: bfloat16 [2048, 2048], P(None, 'head'), may hold values from -0.125 to 0.125
- w_key: bfloat16 [2048, 2048], P(None, 'head'), may hold values from -0.125 to 0.125
- w_value: bfloat16 [2048, 2048], P(None, 'head'), may hold values from -0.125 to 0.125
- w_out: bfloat16 [2048, 2048], P('head'), may hold values from -0.125 to 0.125
- norm_gain: float32 [2048], P('head'), may hold values from 0.5 to 1.5
- forget_rate: float32 [8192, 16], P('seq', 'head'), may hold values from 0 to 2, as said below
- routing: int32 [128, 16, 2], P('seq', 'head'), may hold values from 0 to 7, all different within a row
- memory_blend_share: float32 [128, 16, 2], P('seq', 'head'), may hold values from 0.25 to 1
Outputs:
- mixed: bfloat16 [8192, 2048], P(('seq', 'head'))
The draws below stay inside these ranges and needn't reach their ends.
Inputs may be any that keep to these rules, and one draw needn't show every extreme that they name: `routing`: each block and head names 2 different memories. `forget_rate`: positive rates.
All inputs are finite; a program needn't handle non-finite values.
Results may differ from the reference program's by a relative error of at most 0.03.
Values may be sent and summed in bfloat16 or wider, within the bound.
A program may use at most 128 MiB of HBM per device.

```python
import math
import jax
import jax.numpy as jnp
from jax import lax

D = 2048
ATTENTION_GROUPS = 16
HD = 128
M = 8
TOP = 2
CH = 64
TOKENS = 8192
BLOCKS = 128


def draw_forget_rate(key, part):
    quick_seed_state = jax.random.fold_in(key, 11)
    key_jitter = jax.random.fold_in(key, 12)
    key_spots = jax.random.fold_in(key, 13)
    spell_seed_state = jax.random.fold_in(key, 14)
    writes = TOKENS * TOP / M
    fast_share = 5
    is_fast = jax.random.randint(quick_seed_state, (ATTENTION_GROUPS,), 0, 10) < fast_share
    base = jnp.where(is_fast, 0.025, 0.25 / writes)
    jitter = jnp.exp(jax.random.uniform(key_jitter, (TOKENS, ATTENTION_GROUPS), jnp.float32, -math.log(2.0), math.log(2.0)))
    retention_fades = base[None, :] * jitter
    spots = jax.random.randint(key_spots, (3, ATTENTION_GROUPS), 0, TOKENS)
    spell_durations = jax.random.uniform(spell_seed_state, (3, ATTENTION_GROUPS), jnp.float32, 0.22, 0.45)
    memory_selection_tally = jnp.arange(TOKENS)[:, None, None] == spots[None, :, :]
    retention_fades = retention_fades + jnp.sum(jnp.where(memory_selection_tally, spell_durations[None, :, :], 0.0), axis=1)
    return retention_fades.astype(jnp.float32)


def block_levels(rng, shape, pieces, least, top_value):
    level, own = 1.0, jax.random.fold_in(rng, 6)
    for position, parts in pieces:
        heights = jnp.exp(jax.random.uniform(jax.random.fold_in(own, position), (parts,), jnp.float32, least / len(pieces), top_value / len(pieces)))
        level = level * jnp.repeat(heights, shape[position] // parts).reshape([-1 if axis == position else 1 for axis in range(len(shape))])
    return level


def choose_distinct(stream_key, rows, count, top, lift):
    sequence = jax.random.permutation(jax.random.fold_in(stream_key, 1), count)
    pull = sequence
    for power in range(3):
        pull = pull * pull // count
    pull = pull * lift // count
    tickets = jax.random.randint(jax.random.fold_in(stream_key, 2), (rows, count), 0, 4096) + pull
    fixed_rows = jax.random.permutation(jax.random.fold_in(stream_key, 3), rows)[jnp.arange(count) % rows]
    tickets = jnp.where(jnp.arange(rows)[:, None] == fixed_rows[None, :], 1 << 14, tickets)
    score = tickets * count + jnp.arange(count)
    return lax.top_k(score.astype(jnp.int32), top)[1].astype(jnp.int32)


def scatter_about(key, dims, spread, bound, pieces=(), held_as=jnp.bfloat16):
    values = spread * jax.random.normal(key, dims, jnp.float32)
    if pieces:
        values = values * block_levels(key, dims, pieces, -0.22, 0.18)
    return jnp.clip(values, -bound, bound).astype(held_as)


def setup_inputs(seed: int = 0) -> dict:
    splits = jax.random.split(jax.random.key(seed), 10)
    tokens = scatter_about(splits[0], (TOKENS, D), 1.0, 6.0, ((0, 8),))
    w_query = scatter_about(splits[1], (D, ATTENTION_GROUPS * HD), D ** -0.5, 0.125, ((1, 4),))
    w_key = scatter_about(splits[2], (D, ATTENTION_GROUPS * HD), D ** -0.5, 0.125, ((1, 4),))
    w_value = scatter_about(splits[3], (D, ATTENTION_GROUPS * HD), D ** -0.5, 0.125, ((1, 4),))
    w_out = scatter_about(splits[4], (ATTENTION_GROUPS * HD, D), (ATTENTION_GROUPS * HD) ** -0.5, 0.125, ((0, 4),))
    norm_gain = jnp.clip(1.0 + 0.1 * jax.random.normal(splits[5], (ATTENTION_GROUPS * HD,), jnp.float32), 0.5, 1.5)
    forget_rate = draw_forget_rate(jax.random.fold_in(splits[9], 71), 0)
    routing = choose_distinct(splits[7], BLOCKS * ATTENTION_GROUPS, M, TOP, 2048).reshape((BLOCKS, ATTENTION_GROUPS, TOP))
    memory_blend_share = jnp.clip(0.25 + 0.75 * jax.random.uniform(splits[8], (BLOCKS, ATTENTION_GROUPS, TOP), jnp.float32) ** block_levels(splits[8], (BLOCKS, ATTENTION_GROUPS, TOP), ((0, 8), (1, 4)), -0.2, 0.2), 0.25, 1.0)
    return {"tokens": tokens, "w_query": w_query, "w_key": w_key, "w_value": w_value, "w_out": w_out, "norm_gain": norm_gain, "forget_rate": forget_rate, "routing": routing, "memory_blend_share": memory_blend_share}


HIGH = lax.Precision.HIGHEST

def block_step(memory, inputs):
    query, key_raw, value_raw, retention_fades, chosen, weights = inputs
    heads_all = retention_fades.shape[1]
    query = query.astype(jnp.float32).reshape(CH, heads_all, HD).transpose(1, 0, 2)
    key_rows = key_raw.astype(jnp.float32).reshape(CH, heads_all, HD).transpose(1, 0, 2)
    key_rows = key_rows * lax.rsqrt(lax.optimization_barrier(jnp.sum(key_rows * key_rows, axis=-1, keepdims=True)) + 1e-06)
    key_rows = key_rows.astype(jnp.bfloat16).astype(jnp.float32)
    value_rows = value_raw.astype(jnp.float32).reshape(CH, heads_all, HD).transpose(1, 0, 2)
    cumul = jnp.cumsum(-retention_fades.transpose(1, 0), axis=1)
    block_end = cumul[:, -1]
    positions = jnp.arange(CH)
    causal = positions[:, None] >= positions[None, :]
    gaps = cumul[:, :, None] - cumul[:, None, :]
    decays = jnp.where(causal, jnp.exp(jnp.where(causal, gaps, 0.0)), 0.0)
    scores = jnp.einsum('hqd,hkd->hqk', query, key_rows, precision=HIGH)
    weighted = (scores * decays).astype(jnp.bfloat16).astype(jnp.float32)
    within = jnp.einsum('hqk,hkd->hqd', weighted, value_rows, precision=HIGH)
    one_hot = (chosen[:, :, None] == jnp.arange(M)[None, None, :]).astype(jnp.float32)
    routed = lax.optimization_barrier(jnp.sum(one_hot, axis=1))
    mix_weight = lax.optimization_barrier(jnp.sum(weights[:, :, None] * one_hot, axis=1))
    mixed_state = jnp.einsum('hm,hmde->hde', mix_weight, memory, precision=HIGH)
    carried_part = jnp.exp(cumul)[:, :, None] * jnp.einsum('hqd,hde->hqe', query, mixed_state, precision=HIGH)
    attended_output = carried_part + lax.optimization_barrier(jnp.sum(weights, axis=1))[:, None, None] * within
    scaled_keys = key_rows * jnp.exp(block_end[:, None] - cumul)[:, :, None]
    scaled_keys = scaled_keys.astype(jnp.bfloat16).astype(jnp.float32)
    written = jnp.einsum('hsd,hse->hde', scaled_keys, value_rows, precision=HIGH)
    factor = jnp.where(routed > 0, jnp.exp(block_end)[:, None], 1.0)
    memory = memory * factor[:, :, None, None] + routed[:, :, None, None] * written[:, None]
    return (memory, attended_output.transpose(1, 0, 2))

def reference(tokens, w_query, w_key, w_value, w_out, norm_gain, forget_rate, routing, memory_blend_share):
    query = jnp.dot(tokens, w_query, preferred_element_type=jnp.float32).astype(jnp.bfloat16)
    key_raw = jnp.dot(tokens, w_key, preferred_element_type=jnp.float32).astype(jnp.bfloat16)
    value_raw = jnp.dot(tokens, w_value, preferred_element_type=jnp.float32).astype(jnp.bfloat16)
    num_blocks = TOKENS // CH
    inputs = (query.reshape(num_blocks, CH, ATTENTION_GROUPS * HD), key_raw.reshape(num_blocks, CH, ATTENTION_GROUPS * HD), value_raw.reshape(num_blocks, CH, ATTENTION_GROUPS * HD), forget_rate.reshape(num_blocks, CH, ATTENTION_GROUPS), routing, memory_blend_share)
    memory = jnp.zeros((ATTENTION_GROUPS, M, HD, HD), jnp.float32)
    memory, attended_output = lax.scan(block_step, memory, inputs)
    attended_output = attended_output.reshape(TOKENS, ATTENTION_GROUPS, HD)
    normed = attended_output * lax.rsqrt(lax.optimization_barrier(jnp.mean(attended_output * attended_output, axis=-1, keepdims=True)) + 1e-06)
    normed = (normed * norm_gain.reshape(ATTENTION_GROUPS, HD)).astype(jnp.bfloat16).reshape(TOKENS, ATTENTION_GROUPS * HD)
    return jnp.dot(normed, w_out, preferred_element_type=jnp.float32).astype(jnp.bfloat16)
```

```python
import jax
import jax.numpy as jnp
from jax import lax
from jax.experimental import pallas as pl
from jax.experimental.pallas import tpu as pltpu
from jax.sharding import PartitionSpec as P

HD = 128
M = 8
CH = 64
TILE = 256
SUB = 2
WAIT_SLOTS = 4
HOP_SLOTS = 3

HIGHEST = lax.Precision.HIGHEST
MESH = pl.DeviceIdType.MESH
VMEM = pltpu.VMEM
DMA = pltpu.SemaphoreType.DMA
LIMIT = 64 * 1024 * 1024 - 128 * 1024
BF = jnp.bfloat16
F32 = jnp.float32


def aligned(start, step):
    return pl.multiple_of(start, step)


def dot(a, b, **kw):
    return jnp.dot(a, b, preferred_element_type=F32, **kw)


def layer_kernel(
    rates,
    routing,
    shares,
    gain,
    tokens,
    w_query,
    w_key,
    w_value,
    w_out,
    out,
    tok,
    wkv,
    wq,
    q,
    kt,
    ktf,
    v,
    ks,
    memb,
    p1in,
    zin,
    zout,
    yout,
    sin,
    rowbuf,
    cum,
    tail,
    endr,
    ei_ref,
    e_ref,
    sh_ref,
    wrow,
    prod,
    prodpar,
    coef,
    cr,
    cb,
    qs,
    intra,
    fin,
    exch,
    wfull,
    oacc,
    tok_sem,
    wkv_sem,
    wq_sem,
    own_sem,
    prod_sem,
    p1_sem,
    z_sem,
    y_sem,
    row_sem,
    twin_sem,
    x_sem,
    xt_sem,
    zw_sem,
    zt_sem,
):
    size, me = lax.axis_size("seq"), lax.axis_index("seq")
    groups, mine = lax.axis_size("head"), lax.axis_index("head")
    heads, rows_all = rates.shape
    depth = tokens.shape[1]
    blocks = rows_all // CH
    tiles = rows_all // TILE
    per_tile = TILE // CH
    own_rows = rows_all // groups
    planes = size // 2
    chips = groups // 2
    parity = lax.rem(me, 2)
    plane = lax.div(me, 2)
    even = lax.rem(plane, 2)
    partner = me + 1 - 2 * parity
    zmate = me + 2 - 4 * even
    twin = mine + 1 - 2 * lax.rem(mine, 2)
    units = heads * SUB
    column_rows = M * HD // 2
    unit_rows = column_rows // SUB
    half = HD // 2
    barrier = pltpu.get_barrier_semaphore()

    def tok_copy(i):
        rows = pl.ds(aligned(i * TILE, TILE), TILE)
        return pltpu.make_async_copy(tokens.at[rows, :], tok.at[rows, :], tok_sem.at[i])

    def wkv_copy(h, side):
        cols = pl.ds(aligned(h * HD, HD), HD)
        source = w_value if side else w_key
        return pltpu.make_async_copy(
            source.at[:, cols],
            wkv.at[h, :, side * HD : (side + 1) * HD],
            wkv_sem.at[h, side],
        )

    def wq_copy(i):
        cols = pl.ds(aligned(i * 2 * HD, 2 * HD), 2 * HD)
        return pltpu.make_async_copy(w_query.at[:, cols], wq.at[i], wq_sem.at[i])

    def block_of(owner):
        return pl.ds(aligned(owner * HD, HD), HD)

    def half_of(owner, side):
        return pl.ds(aligned(owner * HD + side * half, half), half)

    own_copy = pltpu.make_async_copy(w_out, wfull.at[:, block_of(mine), :], own_sem)

    def seq_copy(src, dst, send, recv, to):
        return pltpu.make_async_remote_copy(
            src_ref=src,
            dst_ref=dst,
            send_sem=send,
            recv_sem=recv,
            device_id={"seq": to},
            device_id_type=MESH,
        )

    def head_copy(src, dst, send, recv, to):
        return pltpu.make_async_remote_copy(
            src_ref=src,
            dst_ref=dst,
            send_sem=send,
            recv_sem=recv,
            device_id={"head": to},
            device_id_type=MESH,
        )

    prod_copy = seq_copy(prod, prodpar, prod_sem.at[0], prod_sem.at[1], partner)

    def twin_copy(owner):
        return head_copy(
            w_out, wfull.at[:, block_of(owner), :], twin_sem.at[0], twin_sem.at[1], twin
        )

    def x_send(k, h):
        to = lax.rem(mine + 2 * k, groups)
        return head_copy(
            w_out.at[h, pl.ds(aligned(even * half, half), half), :],
            wfull.at[h, half_of(mine, even), :],
            x_sem.at[0, k, h],
            x_sem.at[1, k, h],
            to,
        )

    def x_recv(k, h):
        source = lax.rem(mine + groups - 2 * k, groups)
        place = wfull.at[h, half_of(source, even), :]
        return head_copy(place, place, x_sem.at[0, k, h], x_sem.at[1, k, h], source)

    def xt_copy(k, h, base):
        source = lax.rem(base + groups - 2 * k, groups)
        place = wfull.at[h, half_of(source, even), :]
        return head_copy(place, place, xt_sem.at[0, k, h], xt_sem.at[1, k, h], twin)

    def zw_copy(k, h, side):
        source = lax.rem(mine + groups - 2 * k, groups)
        place = wfull.at[h, half_of(source, side), :]
        return seq_copy(place, place, zw_sem.at[0, k, h], zw_sem.at[1, k, h], zmate)

    def zt_copy(k, h, base):
        source = lax.rem(base + groups - 2 * k, groups)
        place = wfull.at[h, half_of(source, 1 - even), :]
        return head_copy(place, place, zt_sem.at[0, k, h], zt_sem.at[1, k, h], twin)

    def p1_copy(u):
        h, sub = lax.div(u, SUB), lax.rem(u, SUB)
        rows = pl.ds(aligned((1 - parity) * column_rows + sub * unit_rows, unit_rows), unit_rows)
        return seq_copy(
            memb.at[h, rows, :], p1in.at[u], p1_sem.at[0, u], p1_sem.at[1, u], partner
        )

    def z_copy(u):
        return seq_copy(zout.at[u], zin.at[u], z_sem.at[0, u], z_sem.at[1, u], me + 2)

    def y_copy(u, side):
        h, sub = lax.div(u, SUB), lax.rem(u, SUB)
        rows = pl.ds(aligned(side * column_rows + sub * unit_rows, unit_rows), unit_rows)
        return seq_copy(yout.at[u], sin.at[h, rows, :], y_sem.at[0, u], y_sem.at[1, u], partner)

    def rows_of(owner):
        return pl.ds(aligned(owner * own_rows, own_rows), own_rows)

    def row_send(h, k):
        to = lax.rem(mine + k, groups)
        return head_copy(
            fin.at[h, rows_of(to), :],
            exch.at[h, :, block_of(mine)],
            row_sem.at[0, h, to],
            row_sem.at[1, h, mine],
            to,
        )

    def row_recv(h, k):
        source = lax.rem(mine + k, groups)
        return head_copy(
            fin.at[h, rows_of(source), :],
            exch.at[h, :, block_of(source)],
            row_sem.at[0, h, source],
            row_sem.at[1, h, source],
            source,
        )

    def loop(n, body):
        def step(i, carry):
            body(i)
            return carry

        lax.fori_loop(0, n, step, 0)

    for side in range(2):
        wkv_copy(0, side).start()
    for i in range(tiles):
        tok_copy(i).start()
    for h in range(1, heads):
        for side in range(2):
            wkv_copy(h, side).start()
    for i in range(heads // 2):
        wq_copy(i).start()

    pl.semaphore_signal(barrier, 1, device_id={"seq": partner}, device_id_type=MESH)

    @pl.when(plane > 0)
    def _():
        pl.semaphore_signal(barrier, 1, device_id={"seq": me - 2}, device_id_type=MESH)

    @pl.when(plane < planes - 1)
    def _():
        pl.semaphore_signal(barrier, 1, device_id={"seq": me + 2}, device_id_type=MESH)

    for k in range(1, groups):
        pl.semaphore_signal(
            barrier, 1, device_id={"head": lax.rem(mine + k, groups)}, device_id_type=MESH
        )

    lane = lax.broadcasted_iota(jnp.int32, (heads, rows_all), 1)
    spot = lax.rem(lane, CH)
    rate = rates[...]
    total = -rate
    later = -rate
    step = 1
    while step < CH:
        total = total + jnp.where(spot >= step, pltpu.roll(total, step, 1), 0.0)
        later = later + jnp.where(
            spot < CH - step, pltpu.roll(later, rows_all - step, 1), 0.0
        )
        step *= 2
    later = later + rate
    rowbuf[...] = jnp.zeros_like(rowbuf)
    rowbuf[0:heads, :] = total
    for h in range(heads):
        cum[h] = total[h : h + 1]
        tail[h] = jnp.exp(later[h : h + 1])
        endr[h] = (total + later)[h : h + 1]
    columns = jnp.transpose(rowbuf[...])
    for h in range(heads):
        cb[h] = jnp.broadcast_to(columns[:, h : h + 1], (rows_all, HD))

    spread = jnp.where(
        lax.div(lax.broadcasted_iota(jnp.int32, (blocks, rows_all), 1), CH)
        == lax.broadcasted_iota(jnp.int32, (blocks, rows_all), 0),
        1.0,
        0.0,
    )
    wide_lane = lax.broadcasted_iota(jnp.int32, (M, rows_all), 1)
    memory_id = lax.broadcasted_iota(jnp.int32, (M, rows_all), 0).astype(F32)

    for h in range(heads):
        named = dot(routing[h].astype(F32), spread)
        share = dot(shares[h], spread, precision=HIGHEST)
        first = named[0:1] == memory_id
        second = named[1:2] == memory_id
        written = jnp.where(first, 1.0, jnp.where(second, 1.0, 0.0))
        mix = jnp.where(first, share[0:1], jnp.where(second, share[1:2], 0.0))
        own = written * endr[h]
        upto = own
        step = CH
        while step < rows_all:
            upto = upto + jnp.where(wide_lane >= step, pltpu.roll(upto, step, 1), 0.0)
            step *= 2
        whole = upto[:, rows_all - 1 : rows_all]
        ei_ref[h] = upto
        e_ref[h] = upto - own
        sh_ref[h] = mix
        wrow[h] = written * jnp.exp(whole - upto) * tail[h]
        prod[h] = jnp.broadcast_to(jnp.exp(whole), (M, HD))

    waits = 1 + (groups - 1) + jnp.where(plane > 0, 1, 0) + jnp.where(plane < planes - 1, 1, 0)
    pl.semaphore_wait(barrier, waits)
    prod_copy.start()
    for h in range(heads):
        for k in range(1, chips):
            x_send(k, h).start()
    twin_copy(mine).start()
    own_copy.start()

    @pl.when(plane == 0)
    def _():
        zin[...] = jnp.zeros_like(zin)

    def chain_step(u):
        h, sub = lax.div(u, SUB), lax.rem(u, SUB)
        p1_copy(u).wait_recv()

        @pl.when(plane > 0)
        def _():
            z_copy(u).wait_recv()

        start = aligned(parity * column_rows + sub * unit_rows, unit_rows)
        for i in range(unit_rows // HD):
            part = pl.ds(i * HD, HD)
            rows = pl.ds(aligned(start + i * HD, HD), HD)
            m = parity * (M // 2) + sub * (unit_rows // HD) + i
            arrived = zin[u, part, :].astype(F32)
            mine_mem = memb[h, rows, :].astype(F32)
            other_mem = p1in[u, part, :].astype(F32)
            mine_prod = prod[h, pl.ds(m, 1), :]
            other_prod = prodpar[h, pl.ds(m, 1), :]
            lead = parity == 0
            early_mem = jnp.where(lead, mine_mem, other_mem)
            late_mem = jnp.where(lead, other_mem, mine_mem)
            early_prod = jnp.where(lead, mine_prod, other_prod)
            late_prod = jnp.where(lead, other_prod, mine_prod)
            stepped = early_prod * arrived + early_mem
            zout[u, part, :] = (late_prod * stepped + late_mem).astype(BF)
            yout[u, part, :] = jnp.where(lead, stepped, arrived).astype(BF)
            sin[h, rows, :] = jnp.where(lead, arrived, stepped).astype(BF)

        @pl.when(plane < planes - 1)
        def _():
            z_copy(u).start()

        y_copy(u, parity).start()

    def chain_slot(slot):
        u = slot - WAIT_SLOTS - HOP_SLOTS * plane

        @pl.when(jnp.logical_and(u >= 0, u < units))
        def _():
            chain_step(u)

    def service(j):
        if isinstance(j, int) and j >= heads:
            pass
        else:
            for k in range(1, chips):
                x_recv(k, j).wait_recv()
                zw_copy(k, j, even).start()
                xt_copy(k, j, mine).start()
        if j > 0:
            for k in range(1, chips):
                zw_copy(k, j - 1, 1 - even).wait_recv()
                zt_copy(k, j - 1, mine).start()

    def first_stage(h):
        for side in range(2):
            wkv_copy(h, side).wait()

        def project(i):
            @pl.when(h == 0)
            def _():
                tok_copy(i).wait()

            rows = pl.ds(aligned(i * TILE, TILE), TILE)
            both = dot(tok[rows, :], wkv[h])
            v[h, rows, :] = both[:, HD:].astype(BF)
            wide = both[:, :HD].astype(BF).astype(F32)
            keys = wide * lax.rsqrt(jnp.sum(wide * wide, axis=-1, keepdims=True) + 1e-06)
            turned = jnp.transpose(keys.astype(BF).astype(F32))
            ktf[:, rows] = turned
            kt[h, :, rows] = turned.astype(BF)

        loop(tiles, project)
        chain_slot(2 * h)

        @pl.when(h == heads // 2)
        def _():
            service(0)

        @pl.when(h == 0)
        def _():
            prod_copy.wait_recv()

        for m in range(M):
            ks[m * HD : (m + 1) * HD, :] = (ktf[...] * wrow[h, m : m + 1, :]).astype(BF)

        def state(i):
            rows = pl.ds(aligned(i * column_rows, column_rows), column_rows)
            memb[h, rows, :] = dot(ks[rows, :], v[h]).astype(BF)

        loop(2, state)
        for sub in range(SUB):
            p1_copy(h * SUB + sub).start()
        chain_slot(2 * h + 1)

    loop(heads, first_stage)
    slot = 2 * heads
    service(1)

    def query_stage(i):
        wq_copy(i).wait()
        for part in range(2):
            n = rows_all // 2
            rows = slice(part * n, (part + 1) * n)
            both = dot(tok[rows, :], wq[i]).astype(BF)
            q[2 * i, rows, :] = both[:, :HD]
            q[2 * i + 1, rows, :] = both[:, HD:]
            chain_slot(slot + 2 * i + part)

    loop(heads // 2, query_stage)
    slot += heads

    tile_lane = lax.broadcasted_iota(jnp.int32, (CH, TILE), 1)
    tile_row = lax.broadcasted_iota(jnp.int32, (CH, TILE), 0)

    def second_stage(h):
        upto, before, mix, decay = ei_ref[h], e_ref[h], sh_ref[h], tail[h]
        written = jnp.where(mix > 0.0, 1.0, 0.0)
        amount = jnp.sum(mix, axis=0, keepdims=True)
        reads = mix * jnp.exp(before)
        for b in range(blocks):
            at = slice(b * CH, b * CH + 1)
            n = (b // per_tile + 1) * TILE
            coef[h, b] = jnp.broadcast_to(reads[:, at], (M, HD))
            gap = jnp.minimum(before[:, at] - upto[:, :n], 0.0)
            pull = jnp.sum(mix[:, at] * written[:, :n] * jnp.exp(gap), axis=0, keepdims=True)
            position = lax.broadcasted_iota(jnp.int32, (1, n), 1)
            cr[h, b : b + 1, :n] = jnp.where(
                position < b * CH,
                pull * decay[:, :n],
                jnp.where(position < (b + 1) * CH, amount[:, :n], 0.0),
            )

        @pl.when(lax.rem(h, 2) == 1)
        def _():
            j = lax.div(h, 2) + 2

            @pl.when(j < heads)
            def _():
                service_at(j)

        for g in range(tiles):
            rows = slice(g * TILE, (g + 1) * TILE)
            query = q[h, rows, :]
            growth = jnp.exp(cb[h, rows, :])
            acc = jnp.zeros((TILE, HD), F32)
            for t in range(g):
                cols = slice(t * TILE, (t + 1) * TILE)
                scores = dot(query, kt[h, :, cols])
                parts = [
                    (
                        scores[i * CH : (i + 1) * CH]
                        * cr[h, g * per_tile + i : g * per_tile + i + 1, cols]
                    ).astype(BF)
                    for i in range(per_tile)
                ]
                acc = acc + dot(jnp.concatenate(parts, axis=0), v[h, cols, :])
            scores = dot(query, kt[h, :, rows])
            parts = []
            for i in range(per_tile):
                b = g * per_tile + i
                own = cb[h, b * CH : (b + 1) * CH, :]
                col = jnp.concatenate([own] * (TILE // HD), axis=1)
                inside = lax.div(tile_lane, CH) == i
                gap = col - jnp.where(inside, cum[h, :, rows], 0.0)
                factor = jnp.exp(jnp.minimum(gap, 0.0)) * cr[h, b : b + 1, rows]
                factor = jnp.where(tile_lane <= tile_row + i * CH, factor, 0.0)
                parts.append((scores[i * CH : (i + 1) * CH] * factor).astype(BF))
            near = dot(jnp.concatenate(parts, axis=0), v[h, rows, :])
            intra[h, rows, :] = acc * growth + near
            grown = query.astype(F32) * growth
            for i in range(per_tile):
                b = g * per_tile + i
                piece = grown[i * CH : (i + 1) * CH]
                for m in range(M):
                    qs[h, b * CH : (b + 1) * CH, m * HD : (m + 1) * HD] = (
                        piece * coef[h, b, m : m + 1, :]
                    ).astype(BF)
            if g % 2 == 1:
                chain_slot(slot + h * (tiles // 2) + g // 2)

    def service_at(j):
        for k in range(1, chips):
            x_recv(k, j).wait_recv()
            zw_copy(k, j, even).start()
            xt_copy(k, j, mine).start()
            zw_copy(k, j - 1, 1 - even).wait_recv()
            zt_copy(k, j - 1, mine).start()

    loop(heads, second_stage)
    slot += heads * (tiles // 2)
    last_slot = WAIT_SLOTS + HOP_SLOTS * (planes - 1) + units
    if last_slot > slot:
        loop(last_slot - slot, lambda i: chain_slot(slot + i))

    def finish(h):
        for sub in range(SUB):
            y_copy(h * SUB + sub, 1 - parity).wait_recv()

        def piece(k):
            owner = lax.rem(mine + k + 1, groups)
            rows = rows_of(owner)
            whole = intra[h, rows, :] + dot(qs[h, rows, :], sin[h])
            scale = lax.rsqrt(jnp.mean(whole * whole, axis=-1, keepdims=True) + 1e-06)
            fin[h, rows, :] = (whole * scale * gain[h]).astype(BF)

            @pl.when(k < groups - 1)
            def _():
                row_send(h, k + 1).start()

        loop(groups, piece)
        exch[h, :, block_of(mine)] = fin[h, rows_of(mine), :]

    def emit(h, opening, closing):
        for k in range(1, groups):
            row_recv(h, k).wait_recv()
        for k in range(1, chips):
            xt_copy(k, h, twin).wait_recv()
            zt_copy(k, h, twin).wait_recv()
        for part in range(depth // 512):
            cols = slice(part * 512, (part + 1) * 512)
            more = dot(exch[h], wfull[h, :, cols])
            if not opening:
                more = oacc[:, cols] + more
            if closing:
                out[:, cols] = more.astype(BF)
            else:
                oacc[:, cols] = more

    for h in range(heads):
        finish(h)
        if h == 0:
            for k in range(1, chips):
                zw_copy(k, heads - 1, 1 - even).wait_recv()
                zt_copy(k, heads - 1, mine).start()
        if h == 1:
            own_copy.wait()
            twin_copy(twin).wait_recv()
        if h > 0:
            emit(h - 1, h == 1, False)
    emit(heads - 1, heads == 1, True)

    prod_copy.wait_send()
    twin_copy(mine).wait_send()

    def drain_weights(h):
        for k in range(1, chips):
            x_send(k, h).wait_send()
            xt_copy(k, h, mine).wait_send()
            zw_copy(k, h, even).wait_send()
            zt_copy(k, h, mine).wait_send()
        for k in range(1, groups):
            row_send(h, k).wait_send()

    loop(heads, drain_weights)

    def drain_units(u):
        p1_copy(u).wait_send()
        y_copy(u, parity).wait_send()

        @pl.when(plane < planes - 1)
        def _():
            z_copy(u).wait_send()

    loop(units, drain_units)


def per_device(
    tokens, w_query, w_key, w_value, w_out, norm_gain, forget_rate, routing, memory_blend_share
):
    rows, depth = tokens.shape
    width = w_query.shape[1]
    heads = width // HD
    blocks = rows // CH
    groups, size = lax.axis_size("head"), lax.axis_size("seq")
    assert size % 4 == 0 and groups % 2 == 0 and heads % 2 == 0 and rows % TILE == 0
    chips = groups // 2
    own_rows = rows // groups
    units = heads * SUB
    unit_rows = M * HD // 2 // SUB
    vmem = pl.BlockSpec(memory_space=VMEM)
    hbm = pl.BlockSpec(memory_space=pl.ANY)
    return pl.pallas_call(
        layer_kernel,
        out_shape=jax.ShapeDtypeStruct((own_rows, depth), BF),
        in_specs=[vmem] * 4 + [hbm] * 5,
        out_specs=vmem,
        scratch_shapes=[
            VMEM((rows, depth), BF),
            VMEM((heads, depth, 2 * HD), BF),
            VMEM((heads // 2, depth, 2 * HD), BF),
            VMEM((heads, rows, HD), BF),
            VMEM((heads, HD, rows), BF),
            VMEM((HD, rows), F32),
            VMEM((heads, rows, HD), BF),
            VMEM((M * HD, rows), BF),
            VMEM((heads, M * HD, HD), BF),
            VMEM((units, unit_rows, HD), BF),
            VMEM((units, unit_rows, HD), BF),
            VMEM((units, unit_rows, HD), BF),
            VMEM((units, unit_rows, HD), BF),
            VMEM((heads, M * HD, HD), BF),
            VMEM((8, rows), F32),
            VMEM((heads, 1, rows), F32),
            VMEM((heads, 1, rows), F32),
            VMEM((heads, 1, rows), F32),
            VMEM((heads, M, rows), F32),
            VMEM((heads, M, rows), F32),
            VMEM((heads, M, rows), F32),
            VMEM((heads, M, rows), F32),
            VMEM((heads, M, HD), F32),
            VMEM((heads, M, HD), F32),
            VMEM((heads, blocks, M, HD), F32),
            VMEM((heads, blocks, rows), F32),
            VMEM((heads, rows, HD), F32),
            VMEM((heads, rows, M * HD), BF),
            VMEM((heads, rows, HD), F32),
            VMEM((heads, rows, HD), BF),
            VMEM((heads, own_rows, groups * HD), BF),
            VMEM((heads, groups * HD, depth), BF),
            VMEM((own_rows, depth), F32),
            DMA((rows // TILE,)),
            DMA((heads, 2)),
            DMA((heads // 2,)),
            DMA,
            DMA((2,)),
            DMA((2, units)),
            DMA((2, units)),
            DMA((2, units)),
            DMA((2, heads, groups)),
            DMA((2,)),
            DMA((2, chips, heads)),
            DMA((2, chips, heads)),
            DMA((2, chips, heads)),
            DMA((2, chips, heads)),
        ],
        compiler_params=pltpu.CompilerParams(
            collective_id=0, has_side_effects=True, vmem_limit_bytes=LIMIT
        ),
        name="layer",
    )(
        forget_rate.T,
        jnp.transpose(routing, (1, 2, 0)),
        jnp.transpose(memory_blend_share, (1, 2, 0)),
        norm_gain.reshape(heads, 1, HD),
        tokens,
        w_query,
        w_key,
        w_value,
        w_out.reshape(heads, HD, depth),
    )


def solution(mesh):
    placed = (
        P("seq", None),
        P(None, "head"),
        P(None, "head"),
        P(None, "head"),
        P("head", None),
        P("head"),
        P("seq", "head"),
        P("seq", "head", None),
        P("seq", "head", None),
    )
    return jax.shard_map(
        per_device, mesh=mesh, in_specs=placed, out_specs=P(("seq", "head"), None), check_vma=False
    )
```

```python
import jax
import jax.numpy as jnp
from jax import lax
from jax.experimental import pallas as pl
from jax.experimental.pallas import tpu as pltpu
from jax.sharding import PartitionSpec as P

HD = 128
M = 8
CH = 64
TILE = 256
SUB = 2
WAIT_TICKS = 4
HOP_TICKS = 2
PARTS = 2
PIECES = 2

HIGHEST = lax.Precision.HIGHEST
MESH = pl.DeviceIdType.MESH
VMEM = pltpu.VMEM
DMA = pltpu.SemaphoreType.DMA
LIMIT = 64 * 1024 * 1024 - 128 * 1024
BF = jnp.bfloat16
F32 = jnp.float32


def aligned(start, step):
    return pl.multiple_of(start, step)


def dot(a, b, **kw):
    return jnp.dot(a, b, preferred_element_type=F32, **kw)


def layer_kernel(
    rates,
    routing,
    shares,
    gain,
    tokens,
    w_query,
    w_key,
    w_value,
    w_out,
    out,
    tok,
    wkv,
    wq,
    both,
    q,
    kt,
    v,
    ks,
    memb,
    p1in,
    zin,
    zout,
    yout,
    sin,
    rowbuf,
    cum,
    tail,
    endr,
    ei_ref,
    e_ref,
    sh_ref,
    wrow,
    prod,
    prodpar,
    coef,
    cr,
    cb,
    qs,
    intra,
    fin,
    exch,
    wfull,
    oacc,
    tok_sem,
    wkv_sem,
    wq_sem,
    own_sem,
    prod_sem,
    p1_sem,
    z_sem,
    y_sem,
    row_sem,
    twin_sem,
    x_sem,
    xt_sem,
    zw_sem,
    up_sem,
    zt_sem,
):
    size, me = lax.axis_size("seq"), lax.axis_index("seq")
    groups, mine = lax.axis_size("head"), lax.axis_index("head")
    heads, rows_all = rates.shape
    depth = tokens.shape[1]
    blocks = rows_all // CH
    tiles = rows_all // TILE
    per_tile = TILE // CH
    own_rows = rows_all // groups
    planes = size // 2
    chips = groups // 2
    chip, core = lax.div(mine, 2), lax.rem(mine, 2)
    parity = lax.rem(me, 2)
    plane = lax.div(me, 2)
    even = lax.rem(plane, 2)
    partner = me + 1 - 2 * parity
    twin = mine + 1 - 2 * core
    units = heads * SUB
    column_rows = M * HD // 2
    unit_rows = column_rows // SUB
    half = HD // 2
    part_rows = half // PARTS
    piece_rows = part_rows // PIECES
    parts = heads * PARTS
    barrier = pltpu.get_barrier_semaphore()

    def tok_copy(i):
        rows = pl.ds(aligned(i * TILE, TILE), TILE)
        return pltpu.make_async_copy(tokens.at[rows, :], tok.at[rows, :], tok_sem.at[i])

    def wkv_copy(h, side):
        source = w_value if side else w_key
        return pltpu.make_async_copy(
            source.at[:, h * HD : (h + 1) * HD],
            wkv.at[h, :, side * HD : (side + 1) * HD],
            wkv_sem.at[h, side],
        )

    def wq_copy(i):
        return pltpu.make_async_copy(
            w_query.at[:, i * 2 * HD : (i + 1) * 2 * HD], wq.at[i], wq_sem.at[i]
        )

    def block_of(owner):
        return pl.ds(aligned(owner * HD, HD), HD)

    def place(owner, side, part):
        start = owner * HD + side * half + part * part_rows
        return pl.ds(aligned(start, part_rows), part_rows)

    def small_place(owner, side, part, piece):
        start = owner * HD + side * half + part * part_rows + piece * piece_rows
        return pl.ds(aligned(start, piece_rows), piece_rows)

    own_copy = pltpu.make_async_copy(w_out, wfull.at[:, block_of(mine), :], own_sem)

    def seq_copy(src, dst, send, recv, to):
        return pltpu.make_async_remote_copy(
            src_ref=src,
            dst_ref=dst,
            send_sem=send,
            recv_sem=recv,
            device_id={"seq": to},
            device_id_type=MESH,
        )

    def head_copy(src, dst, send, recv, to):
        return pltpu.make_async_remote_copy(
            src_ref=src,
            dst_ref=dst,
            send_sem=send,
            recv_sem=recv,
            device_id={"head": to},
            device_id_type=MESH,
        )

    def prod_copy(h):
        return seq_copy(
            prod.at[h], prodpar.at[h], prod_sem.at[0, h], prod_sem.at[1, h], partner
        )

    def twin_copy(owner):
        return head_copy(
            w_out, wfull.at[:, block_of(owner), :], twin_sem.at[0], twin_sem.at[1], twin
        )

    def behind(base, k):
        return lax.rem(base + groups - 2 * k, groups)

    def x_send(k, j):
        h, part = j // PARTS, j % PARTS
        to = lax.rem(mine + 2 * k, groups)
        start = aligned(even * half + part * part_rows, part_rows)
        return head_copy(
            w_out.at[h, pl.ds(start, part_rows), :],
            wfull.at[h, place(mine, even, part), :],
            x_sem.at[0, k, j],
            x_sem.at[1, k, j],
            to,
        )

    def x_recv(k, j):
        spot = wfull.at[j // PARTS, place(behind(mine, k), even, j % PARTS), :]
        return head_copy(spot, spot, x_sem.at[0, k, j], x_sem.at[1, k, j], behind(mine, k))

    def xt_copy(k, j, base):
        spot = wfull.at[j // PARTS, place(behind(base, k), even, j % PARTS), :]
        return head_copy(spot, spot, xt_sem.at[0, k, j], xt_sem.at[1, k, j], twin)

    def zw_copy(k, j, piece, side, sems, to):
        spot = wfull.at[j // PARTS, small_place(behind(mine, k), side, j % PARTS, piece), :]
        return seq_copy(
            spot, spot, sems.at[k, j, piece], zw_sem.at[1, k, j, piece], to
        )

    def down_copy(k, j, piece):
        return zw_copy(k, j, piece, even, zw_sem.at[0], me - 2)

    def up_copy(k, j, piece):
        return zw_copy(k, j, piece, even, up_sem, me + 2)

    def z_recv(k, j, piece):
        return zw_copy(k, j, piece, 1 - even, zw_sem.at[0], me)

    def zt_copy(k, j, base):
        spot = wfull.at[j // PARTS, place(behind(base, k), 1 - even, j % PARTS), :]
        return head_copy(spot, spot, zt_sem.at[0, k, j], zt_sem.at[1, k, j], twin)

    def p1_copy(u):
        h, sub = lax.div(u, SUB), lax.rem(u, SUB)
        rows = pl.ds(aligned((1 - parity) * column_rows + sub * unit_rows, unit_rows), unit_rows)
        return seq_copy(
            memb.at[h, rows, :], p1in.at[u], p1_sem.at[0, u], p1_sem.at[1, u], partner
        )

    def z_copy(u):
        return seq_copy(zout.at[u], zin.at[u], z_sem.at[0, u], z_sem.at[1, u], me + 2)

    def y_copy(u, side):
        h, sub = lax.div(u, SUB), lax.rem(u, SUB)
        rows = pl.ds(aligned(side * column_rows + sub * unit_rows, unit_rows), unit_rows)
        return seq_copy(yout.at[u], sin.at[h, rows, :], y_sem.at[0, u], y_sem.at[1, u], partner)

    def rows_of(owner):
        return pl.ds(aligned(owner * own_rows, own_rows), own_rows)

    def row_send(h, to):
        return head_copy(
            fin.at[h, rows_of(to), :],
            exch.at[h, :, block_of(mine)],
            row_sem.at[0, h, to],
            row_sem.at[1, h, mine],
            to,
        )

    def row_recv(h, source):
        return head_copy(
            fin.at[h, rows_of(source), :],
            exch.at[h, :, block_of(source)],
            row_sem.at[0, h, source],
            row_sem.at[1, h, source],
            source,
        )

    def loop(start, stop, body):
        def step(i, carry):
            body(i)
            return carry

        lax.fori_loop(start, stop, step, 0)

    for side in range(2):
        wkv_copy(0, side).start()
    for i in range(tiles):
        tok_copy(i).start()
    for h in range(1, heads):
        for side in range(2):
            wkv_copy(h, side).start()
    for i in range(heads // 2):
        wq_copy(i).start()

    pl.semaphore_signal(barrier, 1, device_id={"seq": partner}, device_id_type=MESH)

    @pl.when(plane > 0)
    def _():
        pl.semaphore_signal(barrier, 1, device_id={"seq": me - 2}, device_id_type=MESH)

    @pl.when(plane < planes - 1)
    def _():
        pl.semaphore_signal(barrier, 1, device_id={"seq": me + 2}, device_id_type=MESH)

    for k in range(1, groups):
        pl.semaphore_signal(
            barrier, 1, device_id={"head": lax.rem(mine + k, groups)}, device_id_type=MESH
        )
    waits = 1 + (groups - 1) + jnp.where(plane > 0, 1, 0) + jnp.where(plane < planes - 1, 1, 0)
    pl.semaphore_wait(barrier, waits)
    for j in range(parts):
        for k in range(1, chips):
            x_send(k, j).start()

    lane = lax.broadcasted_iota(jnp.int32, (heads, rows_all), 1)
    spot = lax.rem(lane, CH)
    rate = rates[...]
    total = -rate
    later = -rate
    step = 1
    while step < CH:
        total = total + jnp.where(spot >= step, pltpu.roll(total, step, 1), 0.0)
        later = later + jnp.where(
            spot < CH - step, pltpu.roll(later, rows_all - step, 1), 0.0
        )
        step *= 2
    later = later + rate
    rowbuf[...] = jnp.zeros_like(rowbuf)
    rowbuf[0:heads, :] = total
    for h in range(heads):
        cum[h] = total[h : h + 1]
        tail[h] = jnp.exp(later[h : h + 1])
        endr[h] = (total + later)[h : h + 1]

    spread = jnp.where(
        lax.div(lax.broadcasted_iota(jnp.int32, (blocks, rows_all), 1), CH)
        == lax.broadcasted_iota(jnp.int32, (blocks, rows_all), 0),
        1.0,
        0.0,
    )
    wide_lane = lax.broadcasted_iota(jnp.int32, (M, rows_all), 1)
    memory_id = lax.broadcasted_iota(jnp.int32, (M, rows_all), 0).astype(F32)

    def place_reads(h):
        named = dot(routing[h].astype(F32), spread)
        share = dot(shares[h], spread, precision=HIGHEST)
        first = named[0:1] == memory_id
        second = named[1:2] == memory_id
        written = jnp.where(first, 1.0, jnp.where(second, 1.0, 0.0))
        mix = jnp.where(first, share[0:1], jnp.where(second, share[1:2], 0.0))
        own = written * endr[h]
        upto = own
        step = CH
        while step < rows_all:
            upto = upto + jnp.where(wide_lane >= step, pltpu.roll(upto, step, 1), 0.0)
            step *= 2
        whole = upto[:, rows_all - 1 : rows_all]
        ei_ref[h] = upto
        e_ref[h] = upto - own
        sh_ref[h] = mix
        wrow[h] = written * jnp.exp(whole - upto) * tail[h]
        prod[h] = jnp.broadcast_to(jnp.exp(whole), (M, HD))
        prod_copy(h).start()


    @pl.when(plane == 0)
    def _():
        zin[...] = jnp.zeros_like(zin)

    def chain_step(u):
        h, sub = lax.div(u, SUB), lax.rem(u, SUB)
        p1_copy(u).wait_recv()

        @pl.when(plane > 0)
        def _():
            z_copy(u).wait_recv()

        start = aligned(parity * column_rows + sub * unit_rows, unit_rows)
        for i in range(unit_rows // HD):
            part = pl.ds(i * HD, HD)
            rows = pl.ds(aligned(start + i * HD, HD), HD)
            m = parity * (M // 2) + sub * (unit_rows // HD) + i
            arrived = zin[u, part, :].astype(F32)
            mine_mem = memb[h, rows, :].astype(F32)
            other_mem = p1in[u, part, :].astype(F32)
            mine_prod = prod[h, pl.ds(m, 1), :]
            other_prod = prodpar[h, pl.ds(m, 1), :]
            lead = parity == 0
            early_mem = jnp.where(lead, mine_mem, other_mem)
            late_mem = jnp.where(lead, other_mem, mine_mem)
            early_prod = jnp.where(lead, mine_prod, other_prod)
            late_prod = jnp.where(lead, other_prod, mine_prod)
            stepped = early_prod * arrived + early_mem
            zout[u, part, :] = (late_prod * stepped + late_mem).astype(BF)
            yout[u, part, :] = jnp.where(lead, stepped, arrived).astype(BF)
            sin[h, rows, :] = jnp.where(lead, arrived, stepped).astype(BF)

        @pl.when(plane < planes - 1)
        def _():
            z_copy(u).start()

        y_copy(u, parity).start()

    clock = [0]

    def due(tick):
        ready = tick - WAIT_TICKS - HOP_TICKS * plane
        return jnp.minimum(jnp.maximum(ready, 0), units)

    def chain_to(tick):
        loop(due(clock[0]), due(tick), chain_step)
        clock[0] = tick

    def service(j):
        for k in range(1, chips):
            x_recv(k, j).wait_recv()
            xt_copy(k, j, mine).start()

        @pl.when(plane > 0)
        def _():
            for k in range(1, chips):
                for piece in range(PIECES):
                    down_copy(k, j, piece).start()

    def rise(first, last):
        @pl.when(plane == planes - 2)
        def _():
            for j in range(first, last):
                for k in range(1, chips):
                    for piece in range(PIECES):
                        up_copy(k, j, piece).start()

    def late_service(h):
        for j in range(h * PARTS, (h + 1) * PARTS):
            for k in range(1, chips):
                for piece in range(PIECES):
                    z_recv(k, j, piece).wait_recv()
                zt_copy(k, j, mine).start()

    served = [0]

    def serve(n):
        while served[0] < min(n, parts):
            service(served[0])
            if served[0] < parts // 2 - 1:
                rise(served[0], served[0] + 1)
            served[0] += 1

    def project(h):
        for side in range(2):
            wkv_copy(h, side).wait()
        if h == 0:
            n = rows_all // 2
            for part in range(2):
                for i in range(tiles // 2):
                    tok_copy(part * tiles // 2 + i).wait()
                rows = slice(part * n, (part + 1) * n)
                both[h % 2, rows, :] = dot(tok[rows, :], wkv[h])
        else:
            both[h % 2] = dot(tok[...], wkv[h])

    def remember(h):
        for i in range(rows_all // HD):
            rows = slice(i * HD, (i + 1) * HD)
            v[h, rows, :] = both[h % 2, rows, HD:].astype(BF)
            wide = both[h % 2, rows, :HD].astype(BF).astype(F32)
            keys = wide * lax.rsqrt(jnp.sum(wide * wide, axis=-1, keepdims=True) + 1e-06)
            turned = jnp.transpose(keys.astype(BF).astype(F32))
            kt[h, :, rows] = turned.astype(BF)
            for m in range(M):
                ks[m * HD : (m + 1) * HD, rows] = (turned * wrow[h, m : m + 1, rows]).astype(BF)
        memb[h] = dot(ks[...], v[h]).astype(BF)

    def give(h):
        for sub in range(SUB):
            p1_copy(h * SUB + sub).start()

    def query(i):
        wq_copy(i).wait()
        pair = dot(tok[...], wq[i]).astype(BF)
        q[2 * i] = pair[:, :HD]
        q[2 * i + 1] = pair[:, HD:]

    place_reads(0)
    project(0)
    own_copy.start()
    for h in range(heads):
        if h + 1 < heads:
            project(h + 1)
            place_reads(h + 1)
        else:
            query(0)
        remember(h)
        give(h)
        if h == 0:
            twin_copy(mine).start()
        prod_copy(h).wait_recv()
        chain_to((h + 1) * SUB)
        serve((h + 1) * parts // (2 * heads))
    for i in range(1, heads // 2):
        query(i)
        chain_to(clock[0] + 1)

    tile_lane = lax.broadcasted_iota(jnp.int32, (CH, TILE), 1)
    tile_row = lax.broadcasted_iota(jnp.int32, (CH, TILE), 0)
    columns = jnp.transpose(rowbuf[...])
    for h in range(heads):
        cb[h] = jnp.broadcast_to(columns[:, h : h + 1], (rows_all, HD))

    def tables(h):
        upto, before, mix, decay = ei_ref[h], e_ref[h], sh_ref[h], tail[h]
        written = jnp.where(mix > 0.0, 1.0, 0.0)
        amount = jnp.sum(mix, axis=0, keepdims=True)
        reads = mix * jnp.exp(before)
        for b in range(blocks):
            at = slice(b * CH, b * CH + 1)
            n = (b // per_tile + 1) * TILE
            coef[h, b] = jnp.broadcast_to(reads[:, at], (M, HD))
            gap = jnp.minimum(before[:, at] - upto[:, :n], 0.0)
            pull = jnp.sum(mix[:, at] * written[:, :n] * jnp.exp(gap), axis=0, keepdims=True)
            position = lax.broadcasted_iota(jnp.int32, (1, n), 1)
            cr[h, b : b + 1, :n] = jnp.where(
                position < b * CH,
                pull * decay[:, :n],
                jnp.where(position < (b + 1) * CH, amount[:, :n], 0.0),
            )

    def attend(h, g):
        rows = slice(g * TILE, (g + 1) * TILE)
        query_rows = q[h, rows, :]
        growth = jnp.exp(cb[h, rows, :])
        acc = jnp.zeros((TILE, HD), F32)
        for t in range(g):
            cols = slice(t * TILE, (t + 1) * TILE)
            scores = dot(query_rows, kt[h, :, cols])
            pulls = [
                (
                    scores[i * CH : (i + 1) * CH]
                    * cr[h, g * per_tile + i : g * per_tile + i + 1, cols]
                ).astype(BF)
                for i in range(per_tile)
            ]
            acc = acc + dot(jnp.concatenate(pulls, axis=0), v[h, cols, :])
        scores = dot(query_rows, kt[h, :, rows])
        pulls = []
        for i in range(per_tile):
            b = g * per_tile + i
            own = cb[h, b * CH : (b + 1) * CH, :]
            col = jnp.concatenate([own] * (TILE // HD), axis=1)
            inside = lax.div(tile_lane, CH) == i
            gap = col - jnp.where(inside, cum[h, :, rows], 0.0)
            factor = jnp.exp(jnp.minimum(gap, 0.0)) * cr[h, b : b + 1, rows]
            factor = jnp.where(tile_lane <= tile_row + i * CH, factor, 0.0)
            pulls.append((scores[i * CH : (i + 1) * CH] * factor).astype(BF))
        near = dot(jnp.concatenate(pulls, axis=0), v[h, rows, :])
        intra[h, rows, :] = acc * growth + near
        grown = query_rows.astype(F32) * growth
        for i in range(per_tile):
            b = g * per_tile + i
            piece = grown[i * CH : (i + 1) * CH]
            for m in range(M):
                qs[h, b * CH : (b + 1) * CH, m * HD : (m + 1) * HD] = (
                    piece * coef[h, b, m : m + 1, :]
                ).astype(BF)

    for h in range(heads):
        tables(h)
        for g in range(tiles):
            attend(h, g)
            if g % 2 == 1:
                chain_to(clock[0] + 1)
        serve(parts // 2 + (h + 1) * parts // (2 * heads))

    def finish(h):
        for sub in range(SUB):
            y_copy(h * SUB + sub, 1 - parity).wait_recv()
        for k in range(1, chips + 1):
            to = lax.rem(chip + k, chips)
            n = 2 * own_rows
            rows = pl.ds(aligned(to * n, n), n)
            whole = intra[h, rows, :] + dot(qs[h, rows, :], sin[h])
            scale = lax.rsqrt(jnp.mean(whole * whole, axis=-1, keepdims=True) + 1e-06)
            fin[h, rows, :] = (whole * scale * gain[h]).astype(BF)
            if k < chips:
                row_send(h, 2 * to + core).start()
                row_send(h, 2 * to + 1 - core).start()
            else:
                row_send(h, twin).start()
        exch[h, :, block_of(mine)] = fin[h, rows_of(mine), :]

    def others(body):
        for k in range(1, chips):
            to = lax.rem(chip + k, chips)
            body(2 * to + core)
            body(2 * to + 1 - core)
        body(twin)

    def emit(h):
        others(lambda source: row_recv(h, source).wait_recv())
        for j in range(h * PARTS, (h + 1) * PARTS):
            for k in range(1, chips):
                xt_copy(k, j, twin).wait_recv()
                zt_copy(k, j, twin).wait_recv()
        for part in range(depth // 512):
            cols = slice(part * 512, (part + 1) * 512)
            more = dot(exch[h], wfull[h, :, cols])
            if h > 0:
                more = oacc[:, cols] + more
            if h == heads - 1:
                out[:, cols] = more.astype(BF)
            else:
                oacc[:, cols] = more

    for h in range(heads):
        ahead = min(h + 2, heads) * SUB if h < heads - 2 else units
        chain_to(max(clock[0], WAIT_TICKS + HOP_TICKS * (planes - 1) + ahead))
        if h == 0:
            rise(max(parts // 2 - 1, 0), parts // 2 + 1)
        if h == max(heads - 2, 0):
            rise(parts // 2 + 1, parts)
        finish(h)
        late_service(h)
        if h == 0:
            own_copy.wait()
            twin_copy(twin).wait_recv()
        if h > 0:
            emit(h - 1)
    emit(heads - 1)

    for h in range(heads):
        prod_copy(h).wait_send()
    twin_copy(mine).wait_send()
    for j in range(parts):
        for k in range(1, chips):
            x_send(k, j).wait_send()
            xt_copy(k, j, mine).wait_send()
            zt_copy(k, j, mine).wait_send()

    @pl.when(plane > 0)
    def _():
        for j in range(parts):
            for k in range(1, chips):
                for piece in range(PIECES):
                    down_copy(k, j, piece).wait_send()

    @pl.when(plane == planes - 2)
    def _():
        for j in range(parts):
            for k in range(1, chips):
                for piece in range(PIECES):
                    up_copy(k, j, piece).wait_send()

    for h in range(heads):
        others(lambda to: row_send(h, to).wait_send())

    def drain_units(u):
        p1_copy(u).wait_send()
        y_copy(u, parity).wait_send()

        @pl.when(plane < planes - 1)
        def _():
            z_copy(u).wait_send()

    loop(0, units, drain_units)


def per_device(
    tokens, w_query, w_key, w_value, w_out, norm_gain, forget_rate, routing, memory_blend_share
):
    rows, depth = tokens.shape
    width = w_query.shape[1]
    heads = width // HD
    blocks = rows // CH
    groups, size = lax.axis_size("head"), lax.axis_size("seq")
    assert size % 4 == 0 and groups % 2 == 0 and heads % 2 == 0 and rows % TILE == 0
    chips = groups // 2
    own_rows = rows // groups
    units = heads * SUB
    unit_rows = M * HD // 2 // SUB
    parts = heads * PARTS
    vmem = pl.BlockSpec(memory_space=VMEM)
    hbm = pl.BlockSpec(memory_space=pl.ANY)
    return pl.pallas_call(
        layer_kernel,
        out_shape=jax.ShapeDtypeStruct((own_rows, depth), BF),
        in_specs=[vmem] * 4 + [hbm] * 5,
        out_specs=vmem,
        scratch_shapes=[
            VMEM((rows, depth), BF),
            VMEM((heads, depth, 2 * HD), BF),
            VMEM((heads // 2, depth, 2 * HD), BF),
            VMEM((2, rows, 2 * HD), F32),
            VMEM((heads, rows, HD), BF),
            VMEM((heads, HD, rows), BF),
            VMEM((heads, rows, HD), BF),
            VMEM((M * HD, rows), BF),
            VMEM((heads, M * HD, HD), BF),
            VMEM((units, unit_rows, HD), BF),
            VMEM((units, unit_rows, HD), BF),
            VMEM((units, unit_rows, HD), BF),
            VMEM((units, unit_rows, HD), BF),
            VMEM((heads, M * HD, HD), BF),
            VMEM((8, rows), F32),
            VMEM((heads, 1, rows), F32),
            VMEM((heads, 1, rows), F32),
            VMEM((heads, 1, rows), F32),
            VMEM((heads, M, rows), F32),
            VMEM((heads, M, rows), F32),
            VMEM((heads, M, rows), F32),
            VMEM((heads, M, rows), F32),
            VMEM((heads, M, HD), F32),
            VMEM((heads, M, HD), F32),
            VMEM((heads, blocks, M, HD), F32),
            VMEM((heads, blocks, rows), F32),
            VMEM((heads, rows, HD), F32),
            VMEM((heads, rows, M * HD), BF),
            VMEM((heads, rows, HD), F32),
            VMEM((heads, rows, HD), BF),
            VMEM((heads, own_rows, groups * HD), BF),
            VMEM((heads, groups * HD, depth), BF),
            VMEM((own_rows, depth), F32),
            DMA((rows // TILE,)),
            DMA((heads, 2)),
            DMA((heads // 2,)),
            DMA,
            DMA((2, heads)),
            DMA((2, units)),
            DMA((2, units)),
            DMA((2, units)),
            DMA((2, heads, groups)),
            DMA((2,)),
            DMA((2, chips, parts)),
            DMA((2, chips, parts)),
            DMA((2, chips, parts, PIECES)),
            DMA((chips, parts, PIECES)),
            DMA((2, chips, parts)),
        ],
        compiler_params=pltpu.CompilerParams(
            collective_id=0, has_side_effects=True, vmem_limit_bytes=LIMIT
        ),
        name="layer",
    )(
        forget_rate.T,
        jnp.transpose(routing, (1, 2, 0)),
        jnp.transpose(memory_blend_share, (1, 2, 0)),
        norm_gain.reshape(heads, 1, HD),
        tokens,
        w_query,
        w_key,
        w_value,
        w_out.reshape(heads, HD, depth),
    )


def solution(mesh):
    placed = (
        P("seq", None),
        P(None, "head"),
        P(None, "head"),
        P(None, "head"),
        P("head", None),
        P("head"),
        P("seq", "head"),
        P("seq", "head", None),
        P("seq", "head", None),
    )
    return jax.shard_map(
        per_device, mesh=mesh, in_specs=placed, out_specs=P(("seq", "head"), None), check_vma=False
    )
```
